32 devices in a mesh: dp: 8 (over y, x, core), tensor: 4 (over z).
Axes of the slice: x: 2, y: 2, z: 4, core: 2. Of those that a mesh axis runs over, the one named last changes fastest.
Arguments:
- activations: bfloat16 [4096, 4096], P('dp'), may hold values from -1000 to 1000
- norm_gain: bfloat16 [4096], replicated, may hold values from 0.5 to 1.5
- query_blocks: bfloat16 [128, 32, 4096], P('dp', None, 'tensor'), may hold values from -64 to 64
- query_scales: int32 [128, 1, 4096], P('dp', None, 'tensor'), may hold values from -9 to -5
- key_blocks: bfloat16 [128, 32, 512], P('dp', None, 'tensor'), may hold values from -64 to 64
- key_scales: int32 [128, 1, 512], P('dp', None, 'tensor'), may hold values from -9 to -5
- value_blocks: bfloat16 [128, 32, 512], P('dp', None, 'tensor'), may hold values from -6 to 6
- value_scales: int32 [128, 1, 512], P('dp', None, 'tensor'), may hold values from -9 to -5
- output_blocks: bfloat16 [128, 32, 4096], P('tensor', None, 'dp'), may hold values from -6 to 6
- output_scales: int32 [128, 1, 4096], P('tensor', None, 'dp'), may hold values from -9 to -5
Outputs:
- attended: bfloat16 [4096, 4096], P('dp')
The draws below stay inside these ranges and needn't reach their ends.
All inputs are finite; a program needn't handle non-finite values.
Results may differ from the reference program's by a relative error of at most 0.015.
The reference program's roundings to bfloat16 on the way count: a program that leaves them out, or rounds other values in their place, can miss the bound.
Values may be sent and summed in bfloat16 or wider, within the bound.
No kernel may reach another device: no remote copies, remote signals or barrier semaphores. Data moves between devices by JAX's collectives and lax.ppermute only.
A program may use at most 128 MiB of HBM per device.

```python
import math
import jax
import jax.numpy as jnp
from jax import lax

D = 4096
HEADS = 32
KV_HEADS = 4
HEAD_DIM = 128
BLOCK = 32
SEQ = 256
SEQS = 2
TOKENS = 4096
N_DP = 8
N_TENSOR = 4


def exponent_field(key, shape):
    return jax.random.randint(key, shape, -9, -4).astype(jnp.int32)


def drawn_blocks(key, salt, columns):
    scales = exponent_field(jax.random.fold_in(key, salt), (D // BLOCK, 1, columns))
    values = jnp.clip(jax.random.normal(jax.random.fold_in(key, salt + 1), (D // BLOCK, BLOCK, columns), jnp.float32), -6.0, 6.0)
    return (scales, values)


def draw_query_scales(key, part):
    return drawn_blocks(key, 11, HEADS * HEAD_DIM)[0]


def draw_query_blocks(key, part):
    return drawn_blocks(key, 11, HEADS * HEAD_DIM)[1].astype(jnp.bfloat16)


def draw_key_scales(key, part):
    return drawn_blocks(key, 21, KV_HEADS * HEAD_DIM)[0]


def draw_key_blocks(key, part):
    return drawn_blocks(key, 21, KV_HEADS * HEAD_DIM)[1].astype(jnp.bfloat16)


def draw_activations(key, part):
    row_scale = jnp.exp(jax.random.uniform(jax.random.fold_in(key, 31), (TOKENS, 1), jnp.float32, 0.0, math.log(10.0)))
    column_scale = jnp.exp(jax.random.uniform(jax.random.fold_in(key, 32), (1, D), jnp.float32, 0.0, math.log(10.0)))
    base = jnp.clip(jax.random.normal(jax.random.fold_in(key, 33), (TOKENS, D), jnp.float32), -6.0, 6.0) * row_scale * column_scale
    return base.astype(jnp.bfloat16)


def set_ends(drawn, rng, low, top_value):
    longest = drawn.shape.index(max(drawn.shape))
    spots = []
    for shift in (0, 1):
        where = [jax.random.randint(jax.random.fold_in(rng, axis), (), 0, length) for axis, length in enumerate(drawn.shape)]
        where[longest] = (where[longest] + shift) % drawn.shape[longest]
        spots.append(tuple(where))
    return drawn.at[spots[0]].set(low).at[spots[1]].set(top_value)


def level_of(key, extent, shards, least, high):
    gain = 1.0
    for axis_at, parts in shards:
        heights = jax.random.uniform(jax.random.fold_in(jax.random.fold_in(key, 6), axis_at), (parts,), jnp.float32, least / len(shards), high / len(shards))
        gain = gain * jnp.repeat(jnp.exp(heights), extent[axis_at] // parts).reshape((-1,) + (1,) * (len(extent) - 1 - axis_at))
    return gain


def gaussian(key, shape, width, reach, cuts=(), kind=jnp.bfloat16):
    array = width * jax.random.normal(key, shape, jnp.float32)
    if cuts:
        array = array * level_of(key, shape, cuts, -0.22, 0.18)
    return jnp.clip(array, -reach, reach).astype(kind)


def setup_inputs(seed: int = 0) -> dict:
    splits = jax.random.split(jax.random.key(seed), 11)
    activations = draw_activations(jax.random.fold_in(splits[10], 71), 0)
    norm_gain = jnp.clip(1.0 + 0.1 * jax.random.normal(splits[1], (D,), jnp.float32), 0.5, 1.5).astype(jnp.bfloat16)
    query_blocks = draw_query_blocks(jax.random.fold_in(splits[10], 71), 0)
    query_scales = draw_query_scales(jax.random.fold_in(splits[10], 71), 0)
    key_blocks = draw_key_blocks(jax.random.fold_in(splits[10], 71), 0)
    key_scales = draw_key_scales(jax.random.fold_in(splits[10], 71), 0)
    value_blocks = gaussian(splits[6], (D // BLOCK, BLOCK, KV_HEADS * HEAD_DIM), 1.0, 6.0, ((0, 8), (2, 4)))
    value_scales = set_ends(jax.random.randint(splits[7], (D // BLOCK, 1, KV_HEADS * HEAD_DIM), -9, -4), jax.random.fold_in(splits[7], 1), -9, (-4) - 1).astype(jnp.int32)
    output_blocks = gaussian(splits[8], (HEADS * HEAD_DIM // BLOCK, BLOCK, D), 1.0, 6.0, ((0, 4), (2, 8)))
    output_scales = set_ends(jax.random.randint(splits[9], (HEADS * HEAD_DIM // BLOCK, 1, D), -9, -4), jax.random.fold_in(splits[9], 1), -9, (-4) - 1).astype(jnp.int32)
    return dict(activations=activations, norm_gain=norm_gain, query_blocks=query_blocks, query_scales=query_scales, key_blocks=key_blocks, key_scales=key_scales, value_blocks=value_blocks, value_scales=value_scales, output_blocks=output_blocks, output_scales=output_scales)


EPS = 1e-05
ROPE_BASE = 500000.0

def dequant(blocks, scales):
    factor = jnp.exp2(scales.astype(jnp.float32)).astype(blocks.dtype)
    weight = blocks * factor
    return weight.reshape(weight.shape[0] * weight.shape[1], weight.shape[2])

def rotate_pairs(states, positions):
    half_dim = states.shape[-1] // 2
    frequency = jnp.exp(-math.log(ROPE_BASE) * jnp.arange(half_dim, dtype=jnp.float32) * 2.0 / states.shape[-1])
    angles = positions.astype(jnp.float32)[:, None] * frequency[None, :]
    cosine = jnp.cos(angles)[None, :, None, :]
    sine_part = jnp.sin(angles)[None, :, None, :]
    first = states[..., :half_dim]
    second = states[..., half_dim:]
    return jnp.concatenate([first * cosine - second * sine_part, second * cosine + first * sine_part], axis=-1)

def attend(query_states, key_states, value_states, kv_count):
    tokens_here = query_states.shape[0]
    count = tokens_here // SEQ
    positions = jnp.arange(SEQ, dtype=jnp.int32)
    queries = rotate_pairs(query_states.reshape(count, SEQ, -1, HEAD_DIM), positions).astype(jnp.bfloat16)
    rotated_keys = rotate_pairs(key_states.reshape(count, SEQ, kv_count, HEAD_DIM), positions).astype(jnp.bfloat16)
    value_heads = value_states.astype(jnp.bfloat16).reshape(count, SEQ, kv_count, HEAD_DIM)
    group_size = queries.shape[2] // kv_count
    queries = queries.reshape(count, SEQ, kv_count, group_size, HEAD_DIM)
    scores = jnp.einsum('sqkgd,stkd->skgqt', queries.astype(jnp.float32), rotated_keys.astype(jnp.float32)) * HEAD_DIM ** (-0.5)
    visible = positions[:, None] >= positions[None, :]
    scores = jnp.where(visible, scores, -jnp.inf)
    attn_weights = jax.nn.softmax(scores, axis=-1).astype(jnp.bfloat16)
    context = jnp.einsum('skgqt,stkd->sqkgd', attn_weights.astype(jnp.float32), value_heads.astype(jnp.float32))
    return context.astype(jnp.bfloat16).reshape(tokens_here, -1)

def reference(activations, norm_gain, query_blocks, query_scales, key_blocks, key_scales, value_blocks, value_scales, output_blocks, output_scales):
    query_weight = dequant(query_blocks, query_scales)
    key_weight = dequant(key_blocks, key_scales)
    value_weight = dequant(value_blocks, value_scales)
    output_weight = dequant(output_blocks, output_scales)
    group_rows = SEQS * SEQ
    share = HEADS * HEAD_DIM // N_TENSOR
    kv_share = KV_HEADS * HEAD_DIM // N_TENSOR
    grouped = activations.reshape(N_DP, group_rows, D)

    def one_group(rows):
        wide_rows = rows.astype(jnp.float32)
        inverse = lax.rsqrt(lax.optimization_barrier(jnp.mean(wide_rows * wide_rows, axis=-1, keepdims=True)) + EPS)
        normed = (wide_rows * inverse * norm_gain.astype(jnp.float32)).astype(jnp.bfloat16)
        summed = jnp.zeros((group_rows, D), jnp.float32)
        for member in range(N_TENSOR):
            query_states = jnp.dot(normed, query_weight[:, member * share:(member + 1) * share], preferred_element_type=jnp.float32)
            key_states = jnp.dot(normed, key_weight[:, member * kv_share:(member + 1) * kv_share], preferred_element_type=jnp.float32)
            value_states = jnp.dot(normed, value_weight[:, member * kv_share:(member + 1) * kv_share], preferred_element_type=jnp.float32)
            context = attend(query_states, key_states, value_states, KV_HEADS // N_TENSOR)
            partial_value = jnp.dot(context, output_weight[member * share:(member + 1) * share], preferred_element_type=jnp.float32).astype(jnp.bfloat16)
            partial_value = lax.optimization_barrier(partial_value)
            summed = summed + partial_value.astype(jnp.float32)
        return summed.astype(jnp.bfloat16)
    return lax.map(one_group, grouped).reshape(TOKENS, D)
```

```python
import math

import jax
import jax.numpy as jnp
from jax import lax
from jax.sharding import PartitionSpec as P

HEAD_DIM = 128
SEQ = 256
MAX_PIECES = 8

EPS = 1e-05
ROPE_BASE = 500000.0


def dequant(blocks, scales):
    factor = jnp.exp2(scales.astype(jnp.float32)).astype(blocks.dtype)
    weight = blocks * factor
    return weight.reshape(weight.shape[0] * weight.shape[1], weight.shape[2])


def rotate_pairs(states, positions):
    half_dim = states.shape[-1] // 2
    frequency = jnp.exp(
        -math.log(ROPE_BASE) * jnp.arange(half_dim, dtype=jnp.float32) * 2.0 / states.shape[-1]
    )
    angles = positions.astype(jnp.float32)[:, None] * frequency[None, :]
    cosine = jnp.cos(angles)[None, :, None, :]
    sine_part = jnp.sin(angles)[None, :, None, :]
    first = states[..., :half_dim]
    second = states[..., half_dim:]
    return jnp.concatenate(
        [first * cosine - second * sine_part, second * cosine + first * sine_part], axis=-1
    )


def attend(query_states, key_states, value_states, kv_count):
    tokens_here = query_states.shape[0]
    count = tokens_here // SEQ
    positions = jnp.arange(SEQ, dtype=jnp.int32)
    queries = rotate_pairs(query_states.reshape(count, SEQ, -1, HEAD_DIM), positions).astype(
        jnp.bfloat16
    )
    rotated_keys = rotate_pairs(
        key_states.reshape(count, SEQ, kv_count, HEAD_DIM), positions
    ).astype(jnp.bfloat16)
    value_heads = value_states.astype(jnp.bfloat16).reshape(count, SEQ, kv_count, HEAD_DIM)
    group_size = queries.shape[2] // kv_count
    queries = queries.reshape(count, SEQ, kv_count, group_size, HEAD_DIM)
    scores = jnp.einsum(
        "sqkgd,stkd->skgqt", queries, rotated_keys, preferred_element_type=jnp.float32
    ) * HEAD_DIM ** (-0.5)
    visible = positions[:, None] >= positions[None, :]
    scores = jnp.where(visible, scores, -jnp.inf)
    attn_weights = jax.nn.softmax(scores, axis=-1).astype(jnp.bfloat16)
    context = jnp.einsum(
        "skgqt,stkd->sqkgd", attn_weights, value_heads, preferred_element_type=jnp.float32
    )
    return context.astype(jnp.bfloat16).reshape(tokens_here, -1)


def after(value, *earlier):
    return lax.optimization_barrier((value, *earlier))[0]


def swap(piece, bit, count):
    return lax.ppermute(piece, "dp", [(i, i ^ bit) for i in range(count)])


def spread(halves, count, earlier=()):
    high = [1 << b for b in range(1, count.bit_length() - 1)]
    orders = (high, high[::-1])
    held = [{0: after(half, *earlier) if earlier else half} for half in halves]
    for far in sorted(range(2, count, 2), key=lambda r: (bin(r).count("1"), r)):
        for half, order in zip(held, orders):
            last = [bit for bit in order if far & bit][-1]
            half[far] = swap(half[far ^ last], last, count)
    if count > 1:
        for half in held:
            for far in list(half):
                half[far ^ 1] = swap(half[far], 1, count)
    return held


def to_middle_and_back(part, members):
    where = lax.axis_index("tensor")
    wide = part.astype(jnp.float32)
    total = part
    for hop in range(members // 2 - 1):
        inward = [(hop, hop + 1), (members - 1 - hop, members - 2 - hop)]
        total = (total.astype(jnp.float32) + lax.ppermute(total, "tensor", inward).astype(jnp.float32)).astype(part.dtype)
    left = members // 2 - 1
    across = lax.ppermute(total, "tensor", [(left, left + 1), (left + 1, left)])
    total = (total.astype(jnp.float32) + across.astype(jnp.float32)).astype(part.dtype)
    for hop in reversed(range(members // 2 - 1)):
        outward = [(hop + 1, hop), (members - 2 - hop, members - 1 - hop)]
        outer = lax.ppermute(total, "tensor", outward)
        takes = (where == hop) | (where == members - 1 - hop)
        total = jnp.where(takes, outer, total)
    return total


def whole_normed(activations, norm_gain):
    wide_rows = activations.astype(jnp.float32)
    inverse = lax.rsqrt(jnp.mean(wide_rows * wide_rows, axis=-1, keepdims=True) + EPS)
    return (wide_rows * inverse * norm_gain.astype(jnp.float32)).astype(jnp.bfloat16)


def shards(
    activations,
    norm_gain,
    query_blocks,
    query_scales,
    key_blocks,
    key_scales,
    value_blocks,
    value_scales,
    output_blocks,
    output_scales,
):
    count = lax.axis_size("dp")
    members = lax.axis_size("tensor")
    me = lax.axis_index("dp")
    joint = jnp.concatenate(
        [
            dequant(query_blocks, query_scales),
            dequant(key_blocks, key_scales),
            dequant(value_blocks, value_scales),
        ],
        axis=1,
    )
    output_here = dequant(output_blocks, output_scales)
    normed = whole_normed(activations, norm_gain)
    q_width = query_blocks.shape[2]
    kv_width = key_blocks.shape[2]
    rows = joint.shape[0]
    cols = output_here.shape[1]
    piecewise = count <= MAX_PIECES and count & (count - 1) == 0 and rows % 2 == 0
    if piecewise:
        half_rows = rows // 2
        half_cols = cols // 2
        joint_halves = spread((joint[:half_rows], joint[half_rows:]), count)
        states = 0.0
        for far in sorted(range(count), key=lambda r: (bin(r >> 1).count("1"), r)):
            start = (me ^ far) * rows
            mine = lax.dynamic_slice_in_dim(normed, start, rows, axis=1)
            for side in range(2):
                states = states + jnp.dot(
                    mine[:, side * half_rows : (side + 1) * half_rows],
                    joint_halves[side][far],
                    preferred_element_type=jnp.float32,
                )
        output_halves = spread(
            (output_here[:, :half_cols], output_here[:, half_cols:]),
            count,
            earlier=(joint_halves[0][2], joint_halves[1][4]) if count > 4 else (),
        )
    else:
        states = jnp.dot(
            normed, lax.all_gather(joint, "dp", axis=0, tiled=True), preferred_element_type=jnp.float32
        )
    context = attend(
        states[:, :q_width],
        states[:, q_width : q_width + kv_width],
        states[:, q_width + kv_width :],
        kv_width // HEAD_DIM,
    )
    if not piecewise or members % 2:
        output_weight = lax.all_gather(output_here, "dp", axis=1, tiled=True)
        partial = jnp.dot(context, output_weight, preferred_element_type=jnp.float32)
        return lax.psum(partial.astype(jnp.bfloat16), "tensor")
    attended = jnp.zeros((context.shape[0], cols * count), jnp.bfloat16)
    for far in sorted(range(count), key=lambda r: (bin(r >> 1).count("1"), r)):
        weight = jnp.concatenate([output_halves[0][far], output_halves[1][far]], axis=1)
        partial = jnp.dot(context, weight, preferred_element_type=jnp.float32).astype(jnp.bfloat16)
        total = to_middle_and_back(partial, members)
        attended = lax.dynamic_update_slice_in_dim(attended, total, (me ^ far) * cols, axis=1)
    return attended


def solution(mesh):
    placed = (
        P("dp", None),
        P(),
        P("dp", None, "tensor"),
        P("dp", None, "tensor"),
        P("dp", None, "tensor"),
        P("dp", None, "tensor"),
        P("dp", None, "tensor"),
        P("dp", None, "tensor"),
        P("tensor", None, "dp"),
        P("tensor", None, "dp"),
    )
    return jax.shard_map(
        shards, mesh=mesh, in_specs=placed, out_specs=P("dp", None), check_vma=False
    )
```
